32 devices in a mesh: leaf: 8 (over z, y), chol: 4 (over x, core).
Axes of the slice: x: 2, y: 2, z: 4, core: 2. Of those that a mesh axis runs over, the one named last changes fastest.
Arguments:
- coords: float32 [3, 3072], P(None, 'leaf'), may hold values from 0 to 1
- observed: float32 [16, 3072], P(None, 'leaf'), may hold values from -6 to 6
- cond_index: int32 [8, 512], P('leaf'), may hold values from 0 to 2687, as said below
Outputs:
- cond_mean: float32 [16, 3072], P(None, ('leaf', 'chol'))
- whitened: float32 [16, 3072], P(None, ('leaf', 'chol'))
The draws below stay inside these ranges and needn't reach their ends.
Inputs may be any that keep to these rules, and one draw needn't show every extreme that they name: `cond_index`: slot s of a leaf lies in group s // 128. A group names 128 distinct sites of one leaf. Different groups of a leaf name different leaves, all earlier than the leaf, except groups that name sites of the leaf itself. Every leaf numbered 4 or more names 4 earlier leaves; leaf b below that names b earlier leaves.
All inputs are finite; a program needn't handle non-finite values.
Results may differ from the reference program's by a relative error of at most 0.0003.
Values sent between devices are 32-bit elements; how exact they have to be, the bound alone decides.
No kernel may reach another device: no remote copies, remote signals or barrier semaphores. Data moves between devices by JAX's collectives and lax.ppermute only.
A program may use at most 128 MiB of HBM per device.

```python
import jax
import jax.numpy as jnp
from jax import lax

M = 384
C = 512
S = 16
LEAVES = 8
NPTS = 3072
OWNERS = 4
CAP = 128


def draw_cond_index(key, part):
    base_key = jax.random.fold_in(key, 7)
    favour_key, leaf_key = jax.random.split(base_key)
    favoured = (jax.random.randint(favour_key, (LEAVES,), 0, 8) == 0).astype(jnp.int32)
    leaf_ids = jnp.arange(LEAVES, dtype=jnp.int32)

    def one_leaf(leaf_id, leaf_seed):
        score_key, offset_key = jax.random.split(leaf_seed)
        scores = jax.random.randint(score_key, (LEAVES,), 0, 1000) + 3000 * favoured
        ranked = jnp.where(leaf_ids < leaf_id, scores * LEAVES + leaf_ids, -1 - leaf_ids)
        chosen = jnp.argsort(-ranked)[:OWNERS].astype(jnp.int32)
        owner_ids = jnp.where(chosen < leaf_id, chosen, leaf_id)
        offsets = jax.vmap(lambda group_seed: jax.random.permutation(group_seed, M)[:CAP])(jax.random.split(offset_key, OWNERS))
        return (owner_ids[:, None] * M + offsets.astype(jnp.int32)).reshape(C).astype(jnp.int32)
    return jax.vmap(one_leaf)(leaf_ids, jax.random.split(leaf_key, LEAVES))


def levels(key, extent, cuts, low, top_value):
    gain = 1.0
    for position, parts in cuts:
        draws = jax.random.uniform(jax.random.fold_in(jax.random.fold_in(key, 6), position), (parts,), jnp.float32, low / len(cuts), top_value / len(cuts))
        gain = gain * jnp.repeat(jnp.exp(draws), extent[position] // parts).reshape((-1,) + (1,) * (len(extent) - 1 - position))
    return gain


def gaussian(own_key, extent, scale, bound, cuts=(), kind=jnp.bfloat16):
    factor_of = levels(own_key, extent, cuts, -0.22, 0.18) if cuts else 1.0
    drawn = jax.random.normal(own_key, extent, jnp.float32) * scale * factor_of
    return jnp.minimum(jnp.maximum(drawn, -bound), bound).astype(kind)


def setup_inputs(seed: int = 0) -> dict:
    key_list = jax.random.split(jax.random.key(seed), 4)
    return {
        "coords": jnp.clip(1.0 * jax.random.uniform(key_list[0], (3, NPTS), jnp.float32) ** levels(key_list[0], (3, NPTS), ((1, 8),), -0.2, 0.2), 0.0, 1.0),
        "observed": gaussian(key_list[1], (S, NPTS), 1.0, 6.0, ((1, 8),), jnp.float32),
        "cond_index": draw_cond_index(jax.random.fold_in(key_list[3], 71), 0),
    }


length_scale = 0.3
nugget = 0.2

def covariance(rows_pts, cols_pts, rows_alive, cols_alive, rows_index, cols_index):
    squared = jnp.zeros((rows_pts.shape[1], cols_pts.shape[1]), jnp.float32)
    for axis_id in range(3):
        spacing = rows_pts[axis_id][:, None] - cols_pts[axis_id][None, :]
        squared = squared + spacing * spacing
    kernel = jnp.exp(-jnp.sqrt(squared) / length_scale) * rows_alive[:, None] * cols_alive[None, :]
    on_diagonal = rows_index[:, None] == cols_index[None, :]
    extra = (nugget * cols_alive + 1.0 - cols_alive)[None, :]
    return kernel + jnp.where(on_diagonal, extra, jnp.zeros_like(kernel))

def reference(coords, observed, cond_index):
    joint_order = C + M

    def one_leaf(leaf_id):
        picked = cond_index[leaf_id]
        alive_cond = (picked // M != leaf_id).astype(jnp.float32)
        leaf_start = (leaf_id * M).astype(jnp.int32)
        points = jnp.concatenate([jnp.take(coords, picked, axis=1), lax.dynamic_slice_in_dim(coords, leaf_start, M, 1)], axis=1)
        values = jnp.concatenate([jnp.take(observed, picked, axis=1) * alive_cond[None, :], lax.dynamic_slice_in_dim(observed, leaf_start, M, 1)], axis=1)
        living = jnp.concatenate([alive_cond, jnp.ones((M,), jnp.float32)])
        positions = jnp.arange(joint_order, dtype=jnp.int32)
        matrix = covariance(points, points, living, living, positions, positions)
        factor = jnp.linalg.cholesky(matrix)
        solved = jax.scipy.linalg.solve_triangular(factor, values.T, lower=True)
        cond_part = jnp.dot(factor[C:, :C], solved[:C], precision=lax.Precision.HIGHEST)
        return (cond_part.T, solved[C:].T)
    mean_blocks, white_blocks = lax.map(one_leaf, jnp.arange(LEAVES, dtype=jnp.int32))
    columns = observed.shape[0]
    cond_mean = jnp.transpose(mean_blocks, (1, 0, 2)).reshape(columns, LEAVES * M)
    whitened = jnp.transpose(white_blocks, (1, 0, 2)).reshape(columns, LEAVES * M)
    return (cond_mean, whitened)
```

```python
import functools
import jax
import jax.numpy as jnp
from jax import lax
from jax.experimental import pallas as pl
from jax.experimental.pallas import tpu as pltpu
from jax.sharding import PartitionSpec as P

length_scale = 0.3
nugget = 0.2
B = 128
G = 16
LANES = 128
f32 = jnp.float32
bf16 = jnp.bfloat16


def pieces(x):
    high = x.astype(bf16)
    rest = x - high.astype(f32)
    mid = rest.astype(bf16)
    low = (rest - mid.astype(f32)).astype(bf16)
    return high, mid, low


def kernel(leaf_axis, chol_axis, got_ref, own_ref, idx_ref, mean_ref, white_ref,
           a_ref, d_ref, v_ref, r_ref, w_ref, panel_ref, z_ref, m_ref):
    own = own_ref.shape[1]
    cond = got_ref.shape[1]
    cols = own_ref.shape[0] - 3
    total = cond + own
    nblk = total // B
    nc = cond // B
    leaf_id = lax.axis_index(leaf_axis)
    chol_id = lax.axis_index(chol_axis)

    lane = lax.broadcasted_iota(jnp.int32, (B, B), 1)
    sub = lax.broadcasted_iota(jnp.int32, (B, B), 0)

    row_form, col_form = [], []
    for k in range(nblk):
        if k < nc:
            blk = got_ref[:, k * B:(k + 1) * B]
            alive = (idx_ref[:, k * B:(k + 1) * B] // own != leaf_id).astype(f32)
            vals = blk[3:] * alive
            vals2 = vals
        else:
            blk = own_ref[:, (k - nc) * B:(k - nc + 1) * B]
            alive = jnp.ones((1, B), f32)
            vals = blk[3:]
            vals2 = jnp.zeros_like(vals)
        stack = jnp.concatenate(
            [vals, vals2, blk[:3], alive, jnp.zeros((B - 2 * cols - 4, B), f32)], axis=0)
        t = stack.T
        row_form.append((blk[0:1], blk[1:2], blk[2:3], alive))
        c0 = 2 * cols
        col_form.append(tuple(jnp.broadcast_to(t[:, c0 + i:c0 + i + 1], (B, B)) for i in range(4)))
        a_ref[k * B:(k + 1) * B, total:total + B] = jnp.where(lane < c0, t, 0.0)

    for k in range(nblk):
        cx, cy, cz, ca = col_form[k]
        for c in range(nblk):
            if c < k:
                a_ref[k * B:(k + 1) * B, c * B:(c + 1) * B] = jnp.zeros((B, B), f32)
                continue
            rx, ry, rz, ra = row_form[c]
            dx, dy, dz = cx - rx, cy - ry, cz - rz
            sq = jnp.maximum(dx * dx + dy * dy + dz * dz, 1e-30)
            dist = sq * lax.rsqrt(sq)
            kern = jnp.exp(dist * (-1.0 / length_scale)) * (ca * ra)
            if c == k:
                kern = jnp.where(lane == sub, kern + (nugget * ra + 1.0 - ra), kern)
            a_ref[k * B:(k + 1) * B, c * B:(c + 1) * B] = kern

    lane8 = lax.broadcasted_iota(jnp.int32, (8, B), 1)
    lanec = lax.broadcasted_iota(jnp.int32, (1, B), 1)

    def block_step(k, carry):
        row0 = pl.multiple_of(k * B, B)
        d_ref[...] = a_ref[pl.ds(row0, B), pl.ds(row0, B)]
        for s in range(B // G):
            base = s * G
            halves = G // 8
            for h in range(halves):
                p = d_ref[base + 8 * h:base + 8 * h + 8, :]
                for c in range(8 * h + 8):
                    v_ref[h, c] = jnp.broadcast_to(p[:, base + c:base + c + 1], (8, B))
            S = [[None] * G for _ in range(G)]
            for i in range(G):
                for c in range(i + 1):
                    S[i][c] = jnp.broadcast_to(v_ref[i // 8, c, i % 8:i % 8 + 1, :], (8, B))
            R = [None] * G
            rs = [None] * G
            for i in range(G):
                row = jnp.broadcast_to(d_ref[base + i:base + i + 1, :], (8, B))
                R[i] = jnp.where((lane8 >= base) & (lane8 < base + G),
                                 (lane8 == base + i).astype(f32), row)
            for j in range(G):
                rs[j] = lax.rsqrt(S[j][j])
                R[j] = R[j] * rs[j]
                for i in range(j + 1, G):
                    S[i][j] = S[i][j] * rs[j]
                for i in range(j + 1, G):
                    for c in range(j + 1, i + 1):
                        S[i][c] = S[i][c] - S[i][j] * S[c][j]
                for i in range(j + 1, G):
                    R[i] = R[i] - S[i][j] * R[j]
            for i in range(G):
                r_ref[i:i + 1, :] = R[i][0:1, :]
            rr = r_ref[...]
            w_ref[base:base + G, :] = jnp.where(lanec < base + G, rr, 0.0)
            if s + 1 < B // G:
                h, m, l = pieces(rr)
                left = jnp.concatenate([h, h, m, m, h, l], axis=0)
                right = jnp.concatenate([h, m, h, m, l, h], axis=0)
                upd = lax.dot_general(left[:, base + G:] if False else left, right, (((0,), (0,)), ((), ())),
                                      preferred_element_type=f32)
                keep = (lanec < base) | (lanec >= base + G)
                old = d_ref[base + G:, :]
                d_ref[base + G:, :] = jnp.where(keep, old, 0.0) - upd[base + G:, :]
        panel = jnp.dot(w_ref[...], a_ref[pl.ds(row0, B), :], precision=lax.Precision.HIGHEST,
                        preferred_element_type=f32)
        panel_ref[...] = panel
        panel_ref[:, pl.ds(row0, B)] = jnp.zeros((B, B), f32)
        z_ref[pl.ds(row0, B), :] = panel[:, total:]

        def row_update(j, c):
            r0 = pl.multiple_of(j * B, B)
            upd = lax.dot_general(panel_ref[:, pl.ds(r0, B)], panel_ref[...], (((0,), (0,)), ((), ())),
                                  precision=lax.Precision.HIGHEST, preferred_element_type=f32)
            a_ref[pl.ds(r0, B), :] = a_ref[pl.ds(r0, B), :] - upd
            return c
        lax.fori_loop(k + 1, nblk, row_update, 0)

        @pl.when(k == nc - 1)
        def _():
            m_ref[...] = -a_ref[cond:, total:total + B]
        return carry

    lax.fori_loop(0, nblk, block_step, 0)
    out = mean_ref.shape[1]
    start = pl.multiple_of(chol_id * out, 8)
    pad = jnp.zeros((B - out, B), f32)
    mt = jnp.concatenate([m_ref[pl.ds(start, out), :], pad], axis=0).T
    zt = jnp.concatenate([z_ref[pl.ds(cond + start, out), :], pad], axis=0).T
    mean_ref[...] = mt[cols:2 * cols, :out]
    white_ref[...] = zt[:cols, :out]


def on_device(leaves, chols, coords, observed, cond_index):
    leaf_id = lax.axis_index("leaf")
    own = coords.shape[1]
    cond = cond_index.shape[1]
    cols = observed.shape[0]
    packed = jnp.concatenate([coords, observed], axis=0)
    every = lax.all_gather(packed, "leaf", axis=1, tiled=True)
    got = jnp.take(every, cond_index[0], axis=1)
    out = own // chols
    total = own + cond
    return pl.pallas_call(
        functools.partial(kernel, "leaf", "chol"),
        out_shape=(jax.ShapeDtypeStruct((cols, out), f32),) * 2,
        in_specs=[pl.BlockSpec(memory_space=pltpu.VMEM)] * 3,
        out_specs=(pl.BlockSpec(memory_space=pltpu.VMEM),) * 2,
        scratch_shapes=[
            pltpu.VMEM((total, total + B), f32),
            pltpu.VMEM((B, B), f32),
            pltpu.VMEM((G // 8, G, 8, B), f32),
            pltpu.VMEM((G, B), f32),
            pltpu.VMEM((B, B), f32),
            pltpu.VMEM((B, total + B), f32),
            pltpu.VMEM((total, B), f32),
            pltpu.VMEM((own, B), f32),
        ],
        compiler_params=pltpu.CompilerParams(vmem_limit_bytes=48 << 20),
        name="vecchia",
    )(got, packed, cond_index)


def solution(mesh):
    return jax.shard_map(
        functools.partial(on_device, mesh.shape["leaf"], mesh.shape["chol"]),
        mesh=mesh,
        in_specs=(P(None, "leaf"), P(None, "leaf"), P("leaf", None)),
        out_specs=(P(None, ("leaf", "chol")), P(None, ("leaf", "chol"))),
        check_vma=False,
    )
```

```python
import functools
import jax
import jax.numpy as jnp
from jax import lax
from jax.experimental import pallas as pl
from jax.experimental.pallas import tpu as pltpu
from jax.sharding import PartitionSpec as P

length_scale = 0.3
nugget = 0.2
B = 128
G = 16
LANES = 128
f32 = jnp.float32
bf16 = jnp.bfloat16


def halves(x):
    high = x.astype(bf16)
    return high, (x - high.astype(f32)).astype(bf16)


def kernel(leaf_axis, chol_axis, got_ref, own_ref, idx_ref, mean_ref, white_ref,
           a_ref, d_ref, v_ref, x_ref, w_ref, z_ref, m_ref):
    own = own_ref.shape[1]
    cond = got_ref.shape[1]
    cols = own_ref.shape[0] - 3
    total = cond + own
    nblk = total // B
    nc = cond // B
    leaf_id = lax.axis_index(leaf_axis)
    chol_id = lax.axis_index(chol_axis)

    lane = lax.broadcasted_iota(jnp.int32, (B, B), 1)
    sub = lax.broadcasted_iota(jnp.int32, (B, B), 0)

    row_form, col_form = [], []
    for k in range(nblk):
        if k < nc:
            blk = got_ref[:, k * B:(k + 1) * B]
            alive = (idx_ref[:, k * B:(k + 1) * B] // own != leaf_id).astype(f32)
            vals = blk[3:] * alive
            vals2 = vals
        else:
            blk = own_ref[:, (k - nc) * B:(k - nc + 1) * B]
            alive = jnp.ones((1, B), f32)
            vals = blk[3:]
            vals2 = jnp.zeros_like(vals)
        stack = jnp.concatenate(
            [vals, vals2, blk[:3], alive, jnp.zeros((B - 2 * cols - 4, B), f32)], axis=0)
        t = stack.T
        row_form.append((blk[0:1], blk[1:2], blk[2:3], alive))
        c0 = 2 * cols
        col_form.append(tuple(jnp.broadcast_to(t[:, c0 + i:c0 + i + 1], (B, B)) for i in range(4)))
        a_ref[k * B:(k + 1) * B, total:total + B] = jnp.where(lane < c0, t, 0.0)

    for k in range(nblk):
        cx, cy, cz, ca = col_form[k]
        for c in range(nblk):
            if c < k:
                a_ref[k * B:(k + 1) * B, c * B:(c + 1) * B] = jnp.zeros((B, B), f32)
                continue
            rx, ry, rz, ra = row_form[c]
            dx, dy, dz = cx - rx, cy - ry, cz - rz
            sq = jnp.maximum(dx * dx + dy * dy + dz * dz, 1e-30)
            dist = sq * lax.rsqrt(sq)
            kern = jnp.exp(dist * (-1.0 / length_scale)) * (ca * ra)
            if c == k:
                kern = jnp.where(lane == sub, kern + (nugget * ra + 1.0 - ra), kern)
            a_ref[k * B:(k + 1) * B, c * B:(c + 1) * B] = kern

    lane8 = lax.broadcasted_iota(jnp.int32, (8, B), 1)
    sub8 = lax.broadcasted_iota(jnp.int32, (8, B), 0)

    def spread(x, i):
        return jnp.broadcast_to(x[:, i:i + 1], (8, B))

    def chol8(S, rows):
        scales = []
        for j in range(8):
            r = lax.rsqrt(S[j][j])
            scales.append(r)
            rows[j] = rows[j] * r
            for i in range(j + 1, 8):
                S[i][j] = S[i][j] * r
            for i in range(j + 1, 8):
                for c in range(j + 1, i + 1):
                    S[i][c] = S[i][c] - S[i][j] * S[c][j]
            for i in range(j + 1, 8):
                rows[i] = rows[i] - S[i][j] * rows[j]
        return scales

    def block_step(k, carry):
        row0 = pl.multiple_of(k * B, B)
        d_ref[...] = a_ref[pl.ds(row0, B), pl.ds(row0, B)]
        for s in range(B // G):
            base = s * G
            pivot = (lane8 >= base) & (lane8 < base + G)
            p0 = d_ref[base:base + 8, :]
            p1 = d_ref[base + 8:base + 16, :]
            for c in range(8):
                v_ref[s % 2, 0, c] = spread(p0, base + c)
            V = [spread(p1, base + c) for c in range(16)]
            S = [[jnp.broadcast_to(v_ref[s % 2, 0, c, i:i + 1, :], (8, B)) for c in range(i + 1)] for i in range(8)]
            x0 = jnp.where(pivot, (lane8 == base + sub8).astype(f32), p0)
            x1 = jnp.where(pivot, (lane8 == base + 8 + sub8).astype(f32), p1)
            x_ref[s % 2, 0] = x0
            R = [jnp.broadcast_to(x_ref[s % 2, 0, i:i + 1, :], (8, B)) for i in range(8)]
            scales = chol8(S, R)
            for j in range(8):
                V[j] = V[j] * scales[j]
                for c in range(j + 1, 8):
                    V[c] = V[c] - V[j] * S[c][j]
                v_ref[s % 2, 1, j] = V[j]
                x1 = x1 - V[j] * R[j]
                for c in range(8):
                    V[8 + c] = V[8 + c] - V[j] * jnp.broadcast_to(v_ref[s % 2, 1, j, c:c + 1, :], (8, B))
            for c in range(8):
                v_ref[s % 2, 2, c] = V[8 + c]
            x_ref[s % 2, 1] = x1
            S1 = [[jnp.broadcast_to(v_ref[s % 2, 2, c, i:i + 1, :], (8, B)) for c in range(i + 1)] for i in range(8)]
            R1 = [jnp.broadcast_to(x_ref[s % 2, 1, i:i + 1, :], (8, B)) for i in range(8)]
            chol8(S1, R1)
            R = R + R1
            for i in range(G):
                w_ref[base + i:base + i + 1, :] = R[i][0:1, :]
            for g in range(2 * (s + 1), B // 8):
                index = sub8 + 8 * g
                acc = jnp.where(pivot, 0.0, d_ref[8 * g:8 * g + 8, :])
                for j in range(G):
                    acc = acc - jnp.take_along_axis(R[j], index, axis=1, mode="promise_in_bounds") * R[j]
                d_ref[8 * g:8 * g + 8, :] = acc
        w = jnp.where(lane <= sub, w_ref[...], 0.0)
        wh, wm = halves(w)
        wst = jnp.concatenate([wh, wh, wm], axis=1)
        for t in range(nblk):
            @pl.when(k == t)
            def _(t=t):
                at = a_ref[t * B:(t + 1) * B, (t + 1) * B:]
                ah, am = halves(at)
                panel = jnp.dot(wst, jnp.concatenate([ah, am, ah], axis=0), preferred_element_type=f32)
                z_ref[t * B:(t + 1) * B, :] = panel[:, -B:]
                if t + 1 == nblk:
                    return
                ph, pm = halves(panel)
                right = jnp.concatenate([ph, pm, ph], axis=0)
                left = jnp.concatenate([ph, ph, pm], axis=0)
                for j in range(t + 1, nblk):
                    lo = (j - t - 1) * B
                    upd = lax.dot_general(left[:, lo:lo + B], right[:, lo:], (((0,), (0,)), ((), ())),
                                          preferred_element_type=f32)
                    a_ref[j * B:(j + 1) * B, j * B:] = a_ref[j * B:(j + 1) * B, j * B:] - upd
                if t == nc - 1:
                    m_ref[...] = -a_ref[cond:, total:total + B]
        return carry

    lax.fori_loop(0, nblk, block_step, 0)
    out = mean_ref.shape[1]
    start = pl.multiple_of(chol_id * out, 8)
    pad = jnp.zeros((B - out, B), f32)
    mt = jnp.concatenate([m_ref[pl.ds(start, out), :], pad], axis=0).T
    zt = jnp.concatenate([z_ref[pl.ds(cond + start, out), :], pad], axis=0).T
    mean_ref[...] = mt[cols:2 * cols, :out]
    white_ref[...] = zt[:cols, :out]


def on_device(leaves, chols, coords, observed, cond_index):
    leaf_id = lax.axis_index("leaf")
    own = coords.shape[1]
    cond = cond_index.shape[1]
    cols = observed.shape[0]
    packed = jnp.concatenate([coords, observed], axis=0)
    every = lax.all_to_all(jnp.broadcast_to(packed[None], (leaves,) + packed.shape), "leaf", 0, 0)
    every = jnp.swapaxes(every, 0, 1).reshape(packed.shape[0], leaves * own)
    got = jnp.take(every, cond_index[0], axis=1)
    out = own // chols
    total = own + cond
    return pl.pallas_call(
        functools.partial(kernel, "leaf", "chol"),
        out_shape=(jax.ShapeDtypeStruct((cols, out), f32),) * 2,
        in_specs=[pl.BlockSpec(memory_space=pltpu.VMEM)] * 3,
        out_specs=(pl.BlockSpec(memory_space=pltpu.VMEM),) * 2,
        scratch_shapes=[
            pltpu.VMEM((total, total + B), f32),
            pltpu.VMEM((B, B), f32),
            pltpu.VMEM((2, 3, 8, 8, B), f32),
            pltpu.VMEM((2, 2, 8, B), f32),
            pltpu.VMEM((B, B), f32),
            pltpu.VMEM((total, B), f32),
            pltpu.VMEM((own, B), f32),
        ],
        compiler_params=pltpu.CompilerParams(vmem_limit_bytes=48 << 20),
        name="vecchia",
    )(got, packed, cond_index)


def solution(mesh):
    return jax.shard_map(
        functools.partial(on_device, mesh.shape["leaf"], mesh.shape["chol"]),
        mesh=mesh,
        in_specs=(P(None, "leaf"), P(None, "leaf"), P("leaf", None)),
        out_specs=(P(None, ("leaf", "chol")), P(None, ("leaf", "chol"))),
        check_vma=False,
    )
```

```python
import functools
import jax
import jax.numpy as jnp
from jax import lax
from jax.experimental import pallas as pl
from jax.experimental.pallas import tpu as pltpu
from jax.sharding import PartitionSpec as P

length_scale = 0.3
nugget = 0.2
B = 128
G = 16
LANES = 128
f32 = jnp.float32
bf16 = jnp.bfloat16


def halves(x):
    high = x.astype(bf16)
    return high, (x - high.astype(f32)).astype(bf16)


def thirds(x):
    high = x.astype(bf16)
    rest = x - high.astype(f32)
    mid = rest.astype(bf16)
    return jnp.concatenate([high, mid, (rest - mid.astype(f32)).astype(bf16)], axis=0)


def kernel(leaf_axis, chol_axis, masks, pos_ref, idx_ref, *refs):
    npieces = len(refs) - 10
    piece_refs = refs[:npieces]
    (mean_ref, white_ref, a_ref, d_ref, v_ref, x_ref, w_ref, z_ref, m_ref,
     g_ref) = refs[npieces:]
    own_ref = piece_refs[0]
    own = own_ref.shape[1]
    cond = idx_ref.shape[1]
    cols = own_ref.shape[0] - 3
    total = cond + own
    nblk = total // B
    nc = cond // B
    leaf_id = lax.axis_index(leaf_axis)
    chol_id = lax.axis_index(chol_axis)

    lane = lax.broadcasted_iota(jnp.int32, (B, B), 1)
    sub = lax.broadcasted_iota(jnp.int32, (B, B), 0)

    row_form, col_form = [], []
    if masks:
        i = 0
        for piece in piece_refs:
            tail = g_ref.shape[1] - piece.shape[0]
            for lo in range(0, piece.shape[1], own):
                g_ref[i] = jnp.concatenate([piece[:, lo:lo + own], jnp.zeros((tail, own), f32)], axis=0)
                i += 1
    for k in range(nblk):
        if k < nc:
            if masks:
                far = pos_ref[0, k * B] // own ^ leaf_id
                place = 0
                for i, mask in enumerate(masks):
                    if i:
                        here = jnp.where(chol_id % 2 == 0, mask % 256, mask // 256)
                        place = jnp.where((far == here) & (here > 0), i, place)
                site = idx_ref[:, k * B:(k + 1) * B] % own
                hot = (lax.broadcasted_iota(jnp.int32, (own, B), 0) == site).astype(f32).astype(bf16)
                parts = jnp.dot(thirds(g_ref[place]), hot, preferred_element_type=f32)
                third = parts.shape[0] // 3
                blk = parts[:third] + parts[third:2 * third] + parts[2 * third:]
                blk = blk[:cols + 3]
            else:
                blk = piece_refs[1][:, k * B:(k + 1) * B]
            alive = (idx_ref[:, k * B:(k + 1) * B] // own != leaf_id).astype(f32)
            vals = blk[3:] * alive
            vals2 = vals
        else:
            blk = own_ref[:, (k - nc) * B:(k - nc + 1) * B]
            alive = jnp.ones((1, B), f32)
            vals = blk[3:]
            vals2 = jnp.zeros_like(vals)
        stack = jnp.concatenate(
            [vals, vals2, blk[:3], alive, jnp.zeros((B - 2 * cols - 4, B), f32)], axis=0)
        t = stack.T
        row_form.append((blk[0:1], blk[1:2], blk[2:3], alive))
        c0 = 2 * cols
        col_form.append(tuple(jnp.broadcast_to(t[:, c0 + i:c0 + i + 1], (B, B)) for i in range(4)))
        a_ref[k * B:(k + 1) * B, total:total + B] = jnp.where(lane < c0, t, 0.0)

    for k in range(nblk):
        cx, cy, cz, ca = col_form[k]
        for c in range(nblk):
            if c < k:
                a_ref[k * B:(k + 1) * B, c * B:(c + 1) * B] = jnp.zeros((B, B), f32)
                continue
            rx, ry, rz, ra = row_form[c]
            dx, dy, dz = cx - rx, cy - ry, cz - rz
            sq = jnp.maximum(dx * dx + dy * dy + dz * dz, 1e-30)
            dist = sq * lax.rsqrt(sq)
            kern = jnp.exp(dist * (-1.0 / length_scale)) * (ca * ra)
            if c == k:
                kern = jnp.where(lane == sub, kern + (nugget * ra + 1.0 - ra), kern)
            a_ref[k * B:(k + 1) * B, c * B:(c + 1) * B] = kern

    lane8 = lax.broadcasted_iota(jnp.int32, (8, B), 1)
    sub8 = lax.broadcasted_iota(jnp.int32, (8, B), 0)

    def spread(x, i):
        return jnp.broadcast_to(x[:, i:i + 1], (8, B))

    def chol8(S, rows):
        scales = []
        for j in range(8):
            r = lax.rsqrt(S[j][j])
            scales.append(r)
            rows[j] = rows[j] * r
            for i in range(j + 1, 8):
                S[i][j] = S[i][j] * r
            for i in range(j + 1, 8):
                for c in range(j + 1, i + 1):
                    S[i][c] = S[i][c] - S[i][j] * S[c][j]
            for i in range(j + 1, 8):
                rows[i] = rows[i] - S[i][j] * rows[j]
        return scales

    def block_step(k, carry):
        row0 = pl.multiple_of(k * B, B)
        d_ref[...] = a_ref[pl.ds(row0, B), pl.ds(row0, B)]
        for s in range(B // G):
            base = s * G
            pivot = (lane8 >= base) & (lane8 < base + G)
            p0 = d_ref[base:base + 8, :]
            p1 = d_ref[base + 8:base + 16, :]
            for c in range(8):
                v_ref[s % 2, 0, c] = spread(p0, base + c)
            V = [spread(p1, base + c) for c in range(16)]
            S = [[jnp.broadcast_to(v_ref[s % 2, 0, c, i:i + 1, :], (8, B)) for c in range(i + 1)] for i in range(8)]
            x0 = jnp.where(pivot, (lane8 == base + sub8).astype(f32), p0)
            x1 = jnp.where(pivot, (lane8 == base + 8 + sub8).astype(f32), p1)
            x_ref[s % 2, 0] = x0
            R = [jnp.broadcast_to(x_ref[s % 2, 0, i:i + 1, :], (8, B)) for i in range(8)]
            scales = chol8(S, R)
            for j in range(8):
                V[j] = V[j] * scales[j]
                for c in range(j + 1, 8):
                    V[c] = V[c] - V[j] * S[c][j]
                v_ref[s % 2, 1, j] = V[j]
                x1 = x1 - V[j] * R[j]
                for c in range(8):
                    V[8 + c] = V[8 + c] - V[j] * jnp.broadcast_to(v_ref[s % 2, 1, j, c:c + 1, :], (8, B))
            for c in range(8):
                v_ref[s % 2, 2, c] = V[8 + c]
            x_ref[s % 2, 1] = x1
            S1 = [[jnp.broadcast_to(v_ref[s % 2, 2, c, i:i + 1, :], (8, B)) for c in range(i + 1)] for i in range(8)]
            R1 = [jnp.broadcast_to(x_ref[s % 2, 1, i:i + 1, :], (8, B)) for i in range(8)]
            chol8(S1, R1)
            R = R + R1
            for i in range(G):
                w_ref[base + i:base + i + 1, :] = R[i][0:1, :]
            for g in range(2 * (s + 1), B // 8):
                index = sub8 + 8 * g
                acc = jnp.where(pivot, 0.0, d_ref[8 * g:8 * g + 8, :])
                for j in range(G):
                    acc = acc - jnp.take_along_axis(R[j], index, axis=1, mode="promise_in_bounds") * R[j]
                d_ref[8 * g:8 * g + 8, :] = acc
        w = jnp.where(lane <= sub, w_ref[...], 0.0)
        wh, wm = halves(w)
        wst = jnp.concatenate([wh, wh, wm], axis=1)
        for t in range(nblk):
            @pl.when(k == t)
            def _(t=t):
                at = a_ref[t * B:(t + 1) * B, (t + 1) * B:]
                ah, am = halves(at)
                panel = jnp.dot(wst, jnp.concatenate([ah, am, ah], axis=0), preferred_element_type=f32)
                z_ref[t * B:(t + 1) * B, :] = panel[:, -B:]
                if t + 1 == nblk:
                    return
                ph, pm = halves(panel)
                right = jnp.concatenate([ph, pm, ph], axis=0)
                left = jnp.concatenate([ph, ph, pm], axis=0)
                for j in range(t + 1, nblk):
                    lo = (j - t - 1) * B
                    upd = lax.dot_general(left[:, lo:lo + B], right[:, lo:], (((0,), (0,)), ((), ())),
                                          preferred_element_type=f32)
                    a_ref[j * B:(j + 1) * B, j * B:] = a_ref[j * B:(j + 1) * B, j * B:] - upd
                if t == nc - 1:
                    m_ref[...] = -a_ref[cond:, total:total + B]
        return carry

    lax.fori_loop(0, nblk, block_step, 0)
    out = mean_ref.shape[1]
    start = pl.multiple_of(chol_id * out, 8)
    pad = jnp.zeros((B - out, B), f32)
    mt = jnp.concatenate([m_ref[pl.ds(start, out), :], pad], axis=0).T
    zt = jnp.concatenate([z_ref[pl.ds(cond + start, out), :], pad], axis=0).T
    mean_ref[...] = mt[cols:2 * cols, :out]
    white_ref[...] = zt[:cols, :out]


def on_device(leaves, chols, coords, observed, cond_index):
    own = coords.shape[1]
    cond = cond_index.shape[1]
    cols = observed.shape[0]
    packed = jnp.concatenate([coords, observed], axis=0)
    out = own // chols
    total = own + cond
    bits = leaves.bit_length() - 1
    masks = tuple((1 << t) ^ (1 << (t - 1) if t > 1 else 0) for t in range(bits))
    grouped = 2 * cond // leaves % B == 0
    labels = [0]
    if grouped:
        pieces = [packed]
        def swap(even, odd):
            return [(j * chols + c, (j ^ (odd if c % 2 else even)) * chols + c)
                    for j in range(leaves) for c in range(chols) if (odd if c % 2 else even)]
        plan = [(m + (m >> 1 & 1), m + 1 - (m >> 1 & 1)) for m in range(0, leaves, 2)]
        got = [lax.ppermute(packed, ("leaf", "chol"), swap(*p)) for p in plan]
        cross = [(j, j ^ 1) for j in range(chols)]
        pieces += got + [lax.ppermute(g, "chol", cross) for g in got]
        labels = [0] + [p[0] + 256 * p[1] for p in plan] + [p[1] + 256 * p[0] for p in plan]
        rows = -(-packed.shape[0] // 8) * 8
    else:
        every = packed
        for mask in masks:
            swap = [(j, j ^ mask) for j in range(leaves)]
            every = jnp.concatenate([every, lax.ppermute(every, "leaf", swap)], axis=1)
        far = cond_index[0] // own ^ lax.axis_index("leaf")
        place = jnp.zeros_like(far)
        for bit in range(bits - 1, -1, -1):
            has = (far >> bit) & 1
            place = place + (has << bit)
            far = far ^ (has * masks[bit])
        pieces = [packed, jnp.take(every, place * own + cond_index[0] % own, axis=1)]
        rows = 8
    return pl.pallas_call(
        functools.partial(kernel, "leaf", "chol", tuple(labels) if grouped else ()),
        out_shape=(jax.ShapeDtypeStruct((cols, out), f32),) * 2,
        in_specs=[pl.BlockSpec(memory_space=pltpu.SMEM)]
        + [pl.BlockSpec(memory_space=pltpu.VMEM)] * (1 + len(pieces)),
        out_specs=(pl.BlockSpec(memory_space=pltpu.VMEM),) * 2,
        scratch_shapes=[
            pltpu.VMEM((total, total + B), f32),
            pltpu.VMEM((B, B), f32),
            pltpu.VMEM((2, 3, 8, 8, B), f32),
            pltpu.VMEM((2, 2, 8, B), f32),
            pltpu.VMEM((B, B), f32),
            pltpu.VMEM((total, B), f32),
            pltpu.VMEM((own, B), f32),
            pltpu.VMEM((leaves + 1 if grouped else 1, rows, own), f32),
        ],
        compiler_params=pltpu.CompilerParams(vmem_limit_bytes=48 << 20),
        name="vecchia",
    )(cond_index, cond_index, *pieces)


def solution(mesh):
    return jax.shard_map(
        functools.partial(on_device, mesh.shape["leaf"], mesh.shape["chol"]),
        mesh=mesh,
        in_specs=(P(None, "leaf"), P(None, "leaf"), P("leaf", None)),
        out_specs=(P(None, ("leaf", "chol")), P(None, ("leaf", "chol"))),
        check_vma=False,
    )
```

```python
import functools
import jax
import jax.numpy as jnp
from jax import lax
from jax.experimental import pallas as pl
from jax.experimental.pallas import tpu as pltpu
from jax.sharding import PartitionSpec as P

length_scale = 0.3
nugget = 0.2
B = 128
G = 16
LANES = 128
f32 = jnp.float32
bf16 = jnp.bfloat16


def thirds(x):
    high = x.astype(bf16)
    rest = x - high.astype(f32)
    mid = rest.astype(bf16)
    return high, mid, (rest - mid.astype(f32)).astype(bf16)


def kernel(leaf_axis, chol_axis, masks, pos_ref, idx_ref, *refs):
    npieces = len(refs) - 15
    piece_refs = refs[:npieces]
    (mean_ref, white_ref, a_ref, d_ref, v_ref, x_ref, w_ref, z_ref, m_ref,
     g_ref, f_ref, w3_ref, p3_ref, pt_ref, n_ref) = refs[npieces:]
    own_ref = piece_refs[0]
    own = own_ref.shape[1]
    cond = idx_ref.shape[1]
    cols = own_ref.shape[0] - 3
    total = cond + own
    nblk = total // B
    nc = cond // B
    leaf_id = lax.axis_index(leaf_axis)
    chol_id = lax.axis_index(chol_axis)

    lane = lax.broadcasted_iota(jnp.int32, (B, B), 1)
    sub = lax.broadcasted_iota(jnp.int32, (B, B), 0)

    if masks:
        i = 0
        for piece in piece_refs:
            tail = g_ref.shape[1] - piece.shape[0]
            for lo in range(0, piece.shape[1], own):
                g_ref[i] = jnp.concatenate([piece[:, lo:lo + own], jnp.zeros((tail, own), f32)], axis=0)
                i += 1
    row_form = []
    c0 = 2 * cols
    for k in range(nblk):
        if k < nc:
            if masks:
                far = pos_ref[0, k * B] // own ^ leaf_id
                place = 0
                for i, mask in enumerate(masks):
                    if i:
                        here = jnp.where(chol_id % 2 == 0, mask % 256, mask // 256)
                        place = jnp.where((far == here) & (here > 0), i, place)
                site = idx_ref[:, k * B:(k + 1) * B] % own
                hot = (lax.broadcasted_iota(jnp.int32, (own, B), 0) == site).astype(f32).astype(bf16)
                parts = jnp.dot(jnp.concatenate(thirds(g_ref[place]), axis=0), hot, preferred_element_type=f32)
                third = parts.shape[0] // 3
                blk = parts[:third] + parts[third:2 * third] + parts[2 * third:]
                blk = blk[:cols + 3]
            else:
                blk = piece_refs[1][:, k * B:(k + 1) * B]
            alive = (idx_ref[:, k * B:(k + 1) * B] // own != leaf_id).astype(f32)
            vals = blk[3:] * alive
            vals2 = vals
        else:
            blk = own_ref[:, (k - nc) * B:(k - nc + 1) * B]
            alive = jnp.ones((1, B), f32)
            vals = blk[3:]
            vals2 = jnp.zeros_like(vals)
        stack = jnp.concatenate(
            [vals, vals2, blk[:3], alive, jnp.zeros((B - c0 - 4, B), f32)], axis=0)
        t = stack.T
        f_ref[:, k * B:(k + 1) * B] = jnp.concatenate([blk[:3], alive, jnp.zeros((4, B), f32)], axis=0)
        a_ref[k * B:(k + 1) * B, total:] = t

    def build(k, tiles):
        t = a_ref[k * B:(k + 1) * B, total:]
        cx, cy, cz, ca = (jnp.broadcast_to(t[:, c0 + i:c0 + i + 1], (B, B)) for i in range(4))
        for c in tiles:
            rx, ry, rz, ra = (f_ref[i:i + 1, c * B:(c + 1) * B] for i in range(4))
            dx, dy, dz = cx - rx, cy - ry, cz - rz
            sq = jnp.maximum(dx * dx + dy * dy + dz * dz, 1e-30)
            dist = sq * lax.rsqrt(sq)
            kern = jnp.exp(dist * (-1.0 / length_scale)) * (ca * ra)
            if c == k:
                kern = jnp.where(lane == sub, kern + (nugget * ra + 1.0 - ra), kern)
            a_ref[k * B:(k + 1) * B, c * B:(c + 1) * B] = kern

    lane8 = lax.broadcasted_iota(jnp.int32, (8, B), 1)
    sub8 = lax.broadcasted_iota(jnp.int32, (8, B), 0)
    steps = B // G

    def spread(x, i):
        return jnp.broadcast_to(x[:, i:i + 1], (8, B))

    def row(ref, i):
        return jnp.broadcast_to(ref[i:i + 1, :], (8, B))

    def chol8(S, rows):
        scales = []
        for j in range(0, 8, 2):
            d, low, e = S[j][j], S[j + 1][j], S[j + 1][j + 1]
            det = d * e - low * low
            r = lax.rsqrt(d)
            rd = lax.rsqrt(det)
            q = rd * r
            r1 = q * d
            for i in range(j + 2, 8):
                S[i][j + 1] = (S[i][j + 1] * d - low * S[i][j]) * q
                S[i][j] = S[i][j] * r
            S[j + 1][j] = low * r
            for i in range(j + 2, 8):
                for c in range(j + 2, i + 1):
                    S[i][c] = (S[i][c] - S[i][j] * S[c][j]) - S[i][j + 1] * S[c][j + 1]
            scales += [r, r1]
            rows[j] = rows[j] * r
            rows[j + 1] = (rows[j + 1] - S[j + 1][j] * rows[j]) * r1
            for i in range(j + 2, 8):
                rows[i] = (rows[i] - S[i][j] * rows[j]) - S[i][j + 1] * rows[j + 1]
        return scales
    def pivot_of(s):
        return (lane8 >= s * G) & (lane8 < s * G + G)

    def eliminate(s, R, groups):
        for g in groups:
            index = sub8 + 8 * g
            acc = jnp.where(pivot_of(s), 0.0, d_ref[8 * g:8 * g + 8, :])
            for j in range(G):
                acc = acc - gather(R[j], index) * R[j]
            d_ref[8 * g:8 * g + 8, :] = acc

    def gather(x, index):
        return jnp.take_along_axis(x, index, axis=1, mode="promise_in_bounds")
    def begin(par, p0, p1, base):
        for c in range(8): v_ref[par, 0, c] = spread(p0, base + c)
        for c in range(16): v_ref[par, 3 + c // 8, c % 8] = spread(p1, base + c)
    def chain(s):
        base = s * G; par = s % 2; nxt = 1 - par; pivot = pivot_of(s)
        S = [[row(v_ref.at[par, 0, c], i) for c in range(i + 1)] for i in range(8)]
        V = [v_ref[par, 3 + c // 8, c % 8] for c in range(16)]
        x0 = jnp.where(pivot, (lane8 == base + sub8).astype(f32), d_ref[base:base + 8, :])
        x1 = jnp.where(pivot, (lane8 == base + 8 + sub8).astype(f32), d_ref[base + 8:base + 16, :])
        x_ref[par, 0] = x0
        R = [row(x_ref.at[par, 0], i) for i in range(8)]
        scales = chol8(S, R)
        for j in range(8):
            V[j] = V[j] * scales[j]
            for c in range(j + 1, 8): V[c] = V[c] - V[j] * S[c][j]
            v_ref[par, 1, j] = V[j]
            x1 = x1 - V[j] * R[j]
            for c in range(8): V[8 + c] = V[8 + c] - V[j] * row(v_ref.at[par, 1, j], c)
        for c in range(8): v_ref[par, 2, c] = V[8 + c]
        x_ref[par, 1] = x1
        S1 = [[row(v_ref.at[par, 2, c], i) for c in range(i + 1)] for i in range(8)]
        R1 = [row(x_ref.at[par, 1], i) for i in range(8)]
        more = s + 1 < steps
        if more:
            nb = base + G
            i0, i1 = sub8 + nb, sub8 + nb + 8
            q0 = jnp.where(pivot, 0.0, d_ref[nb:nb + 8, :]); q1 = jnp.where(pivot, 0.0, d_ref[nb + 8:nb + 16, :])
            for j in range(8):
                q0 = q0 - gather(R[j], i0) * R[j]
                q1 = q1 - gather(R[j], i1) * R[j]
            N0 = [spread(q0, nb + c) for c in range(8)]
            N1 = [spread(q1, nb + c) for c in range(16)]
        chol8(S1, R1)
        for i in range(8):
            w_ref[base + i:base + i + 1, :] = R[i][0:1, :]
            w_ref[base + 8 + i:base + 9 + i, :] = R1[i][0:1, :]
        if more:
            for j in range(8):
                m0, m1 = gather(R1[j], i0), gather(R1[j], i1)
                q0 = q0 - m0 * R1[j]
                q1 = q1 - m1 * R1[j]
                n_ref[j, 0] = m0
                n_ref[j, 1] = m1
                for c in range(8):
                    e0, e1 = row(n_ref.at[j, 0], c), row(n_ref.at[j, 1], c)
                    N0[c] = N0[c] - m0 * e0
                    N1[c] = N1[c] - m1 * e0
                    N1[8 + c] = N1[8 + c] - m1 * e1
            d_ref[nb:nb + 8, :] = q0
            d_ref[nb + 8:nb + 16, :] = q1
            for c in range(8): v_ref[nxt, 0, c] = N0[c]
            for c in range(16): v_ref[nxt, 3 + c // 8, c % 8] = N1[c]
    def near2(s):
        R = [row(w_ref, s * G + i) for i in range(G)]
        eliminate(s, R, (2 * s + 4, 2 * s + 5))
    def distant(s):
        lo = (s + 3) * G
        if lo >= B: return
        parts = thirds(w_ref[s * G:s * G + G, :])
        left = jnp.concatenate([parts[i] for i in (0, 0, 1, 1, 0, 2)], axis=0)
        right = jnp.concatenate([parts[i] for i in (0, 1, 0, 1, 2, 0)], axis=0)
        upd = lax.dot_general(left, right, (((0,), (0,)), ((), ())), preferred_element_type=f32)
        keep = (lane8[:1] < s * G) | (lane8[:1] >= s * G + G)
        d_ref[lo:, :] = jnp.where(keep, d_ref[lo:, :], 0.0) - upd[lo:]
    left_order = (0, 0, 1, 1, 0, 2)
    right_order = (0, 1, 0, 1, 2, 0)

    def left_of(parts):
        return jnp.concatenate([parts[i] for i in left_order], axis=1)

    def right_of(parts):
        return jnp.concatenate([parts[i] for i in right_order], axis=0)

    def panel(t, lo, hi):
        left = left_of([w3_ref[i] for i in range(3)])
        right = right_of(thirds(a_ref[t * B:(t + 1) * B, lo * B:hi * B]))
        p = jnp.dot(left, right, preferred_element_type=f32)
        if hi == nblk + 1:
            z_ref[t * B:(t + 1) * B, :] = p[:, -B:]
        if t + 1 == nblk:
            return
        for i, part in enumerate(thirds(p)):
            p3_ref[i, :, lo * B:hi * B] = part
        for c in range(lo, min(hi, nblk)):
            for i, part in enumerate(thirds(p[:, (c - lo) * B:(c - lo + 1) * B].T)):
                pt_ref[i, c * B:(c + 1) * B, :] = part

    def trailing(j, lo, hi):
        left = left_of([pt_ref[i, j * B:(j + 1) * B, :] for i in range(3)])
        right = right_of([p3_ref[i, :, lo * B:hi * B] for i in range(3)])
        return jnp.dot(left, right, preferred_element_type=f32)

    def update(j, lo, hi):
        a_ref[j * B:(j + 1) * B, lo * B:hi * B] = a_ref[j * B:(j + 1) * B, lo * B:hi * B] - trailing(j, lo, hi)

    build(0, (0,))
    d_ref[...] = a_ref[:B, :B]
    always = chol_id >= 0
    for k in range(nblk):
        for s in range(steps):
            @pl.when(always)
            def _(k=k, s=s):
                if s == 0:
                    begin(0, d_ref[0:8, :], d_ref[8:16, :], 0)
                if s and s + 1 < steps:
                    near2(s - 1)
                if s:
                    distant(s - 1)
                if k == 0:
                    if s < nblk:
                        build(s, range(max(s, 1), nblk))
                elif s == 0:
                    panel(k - 1, k + 1, nblk + 1)
                elif k + s - 1 < nblk:
                    j = k + s - 1
                    update(j, max(j, k + 1), nblk + 1)
                chain(s)
        for i, part in enumerate(thirds(jnp.where(lane <= sub, w_ref[...], 0.0))):
            w3_ref[i] = part
        if k == nc:
            m_ref[...] = -a_ref[cond:, total:]
        panel(k, k + 1, k + 2)
        if k + 1 < nblk:
            d_ref[...] = a_ref[(k + 1) * B:(k + 2) * B, (k + 1) * B:(k + 2) * B] - trailing(k + 1, k + 1, k + 2)

    out = mean_ref.shape[1]
    start = pl.multiple_of(chol_id * out, 8)
    pad = jnp.zeros((B - out, B), f32)
    mt = jnp.concatenate([m_ref[pl.ds(start, out), :], pad], axis=0).T
    zt = jnp.concatenate([z_ref[pl.ds(cond + start, out), :], pad], axis=0).T
    mean_ref[...] = mt[cols:2 * cols, :out]
    white_ref[...] = zt[:cols, :out]


def on_device(leaves, chols, coords, observed, cond_index):
    own = coords.shape[1]
    cond = cond_index.shape[1]
    cols = observed.shape[0]
    packed = jnp.concatenate([coords, observed], axis=0)
    out = own // chols
    total = own + cond
    bits = leaves.bit_length() - 1
    masks = tuple((1 << t) ^ (1 << (t - 1) if t > 1 else 0) for t in range(bits))
    grouped = 2 * cond // leaves % B == 0
    labels = [0]
    if grouped:
        pieces = [packed]
        def swap(even, odd):
            return [(j * chols + c, (j ^ (odd if c % 2 else even)) * chols + c)
                    for j in range(leaves) for c in range(chols) if (odd if c % 2 else even)]
        plan = [(m + (m >> 1 & 1), m + 1 - (m >> 1 & 1)) for m in range(0, leaves, 2)]
        got = [lax.ppermute(packed, ("leaf", "chol"), swap(*p)) for p in plan]
        cross = [(j, j ^ 1) for j in range(chols)]
        pieces += got + [lax.ppermute(g, "chol", cross) for g in got]
        labels = [0] + [p[0] + 256 * p[1] for p in plan] + [p[1] + 256 * p[0] for p in plan]
        rows = -(-packed.shape[0] // 8) * 8
    else:
        every = packed
        for mask in masks:
            swap = [(j, j ^ mask) for j in range(leaves)]
            every = jnp.concatenate([every, lax.ppermute(every, "leaf", swap)], axis=1)
        far = cond_index[0] // own ^ lax.axis_index("leaf")
        place = jnp.zeros_like(far)
        for bit in range(bits - 1, -1, -1):
            has = (far >> bit) & 1
            place = place + (has << bit)
            far = far ^ (has * masks[bit])
        pieces = [packed, jnp.take(every, place * own + cond_index[0] % own, axis=1)]
        rows = 8
    return pl.pallas_call(
        functools.partial(kernel, "leaf", "chol", tuple(labels) if grouped else ()),
        out_shape=(jax.ShapeDtypeStruct((cols, out), f32),) * 2,
        in_specs=[pl.BlockSpec(memory_space=pltpu.SMEM)]
        + [pl.BlockSpec(memory_space=pltpu.VMEM)] * (1 + len(pieces)),
        out_specs=(pl.BlockSpec(memory_space=pltpu.VMEM),) * 2,
        scratch_shapes=[
            pltpu.VMEM((total, total + B), f32),
            pltpu.VMEM((B, B), f32),
            pltpu.VMEM((2, 5, 8, 8, B), f32),
            pltpu.VMEM((2, 2, 8, B), f32),
            pltpu.VMEM((B, B), f32),
            pltpu.VMEM((total, B), f32),
            pltpu.VMEM((own, B), f32),
            pltpu.VMEM((leaves + 1 if grouped else 1, rows, own), f32),
            pltpu.VMEM((8, total), f32),
            pltpu.VMEM((3, B, B), bf16),
            pltpu.VMEM((3, B, total + B), bf16),
            pltpu.VMEM((3, total, B), bf16),
            pltpu.VMEM((8, 2, 8, B), f32),
        ],
        compiler_params=pltpu.CompilerParams(vmem_limit_bytes=48 << 20),
        name="vecchia",
    )(cond_index, cond_index, *pieces)


def solution(mesh):
    return jax.shard_map(
        functools.partial(on_device, mesh.shape["leaf"], mesh.shape["chol"]),
        mesh=mesh,
        in_specs=(P(None, "leaf"), P(None, "leaf"), P("leaf", None)),
        out_specs=(P(None, ("leaf", "chol")), P(None, ("leaf", "chol"))),
        check_vma=False,
    )
```

```python
import functools
import jax
import jax.numpy as jnp
from jax import lax
from jax.experimental import pallas as pl
from jax.experimental.pallas import tpu as pltpu
from jax.sharding import PartitionSpec as P

length_scale = 0.3
nugget = 0.2
B = 128
G = 16
LANES = 128
f32 = jnp.float32
bf16 = jnp.bfloat16


def thirds(x):
    high = x.astype(bf16)
    rest = x - high.astype(f32)
    mid = rest.astype(bf16)
    return high, mid, (rest - mid.astype(f32)).astype(bf16)


def kernel(leaf_axis, chol_axis, masks, pos_ref, idx_ref, *refs):
    npieces = len(refs) - 16
    piece_refs = refs[:npieces]
    (mean_ref, white_ref, a_ref, d_ref, v_ref, x_ref, w_ref, z_ref, m_ref,
     g_ref, f_ref, w3_ref, p3_ref, pt_ref, n_ref, q_ref) = refs[npieces:]
    own_ref = piece_refs[0]
    own = own_ref.shape[1]
    cond = idx_ref.shape[1]
    cols = own_ref.shape[0] - 3
    total = cond + own
    nblk = total // B
    nc = cond // B
    leaf_id = lax.axis_index(leaf_axis)
    chol_id = lax.axis_index(chol_axis)

    lane = lax.broadcasted_iota(jnp.int32, (B, B), 1)
    sub = lax.broadcasted_iota(jnp.int32, (B, B), 0)

    if masks:
        i = 0
        for piece in piece_refs:
            tail = g_ref.shape[1] - piece.shape[0]
            for lo in range(0, piece.shape[1], own):
                g_ref[i] = jnp.concatenate([piece[:, lo:lo + own], jnp.zeros((tail, own), f32)], axis=0)
                i += 1
    row_form = []
    c0 = 2 * cols
    for k in range(nblk):
        if k < nc:
            if masks:
                far = pos_ref[0, k * B] // own ^ leaf_id
                place = 0
                for i, mask in enumerate(masks):
                    if i:
                        here = jnp.where(chol_id % 2 == 0, mask % 256, mask // 256)
                        place = jnp.where((far == here) & (here > 0), i, place)
                site = idx_ref[:, k * B:(k + 1) * B] % own
                hot = (lax.broadcasted_iota(jnp.int32, (own, B), 0) == site).astype(f32).astype(bf16)
                parts = jnp.dot(jnp.concatenate(thirds(g_ref[place]), axis=0), hot, preferred_element_type=f32)
                third = parts.shape[0] // 3
                blk = parts[:third] + parts[third:2 * third] + parts[2 * third:]
                blk = blk[:cols + 3]
            else:
                blk = piece_refs[1][:, k * B:(k + 1) * B]
            alive = (idx_ref[:, k * B:(k + 1) * B] // own != leaf_id).astype(f32)
            vals = blk[3:] * alive
            vals2 = vals
            away = (lax.broadcasted_iota(jnp.int32, (1, B), 1) + (k * B + 2)).astype(f32) * 1e3
            pts = jnp.where(alive > 0.5, blk[:3], away)
        else:
            blk = own_ref[:, (k - nc) * B:(k - nc + 1) * B]
            alive = jnp.ones((1, B), f32)
            vals = blk[3:]
            vals2 = jnp.zeros_like(vals)
            pts = blk[:3]
        stack = jnp.concatenate(
            [vals, vals2, pts, jnp.zeros((B - c0 - 3, B), f32)], axis=0)
        t = stack.T
        f_ref[:, k * B:(k + 1) * B] = jnp.concatenate([pts, alive, jnp.zeros((4, B), f32)], axis=0)
        a_ref[k * B:(k + 1) * B, total:] = jnp.where(lane < c0, t, 0.0)
        q_ref[k * B:(k + 1) * B, :] = t

    def build(k, tiles):
        t = q_ref[k * B:(k + 1) * B, :]
        cx, cy, cz = (jnp.broadcast_to(t[:, c0 + i:c0 + i + 1], (B, B)) for i in range(3))
        for c in tiles:
            rx, ry, rz, ra = (f_ref[i:i + 1, c * B:(c + 1) * B] for i in range(4))
            dx, dy, dz = cx - rx, cy - ry, cz - rz
            sq = jnp.maximum(dx * dx + dy * dy + dz * dz, 1e-30)
            kern = jnp.exp2(sq * lax.rsqrt(sq) * (-1.4426950408889634 / length_scale))
            if c == k:
                kern = jnp.where(lane == sub, kern + nugget * ra, kern)
            a_ref[k * B:(k + 1) * B, c * B:(c + 1) * B] = kern

    lane8 = lax.broadcasted_iota(jnp.int32, (8, B), 1)
    sub8 = lax.broadcasted_iota(jnp.int32, (8, B), 0)
    steps = B // G

    def spread(x, i):
        return jnp.broadcast_to(x[:, i:i + 1], (8, B))

    def row(ref, i):
        return jnp.broadcast_to(ref[i:i + 1, :], (8, B))

    def chol8(S, rows):
        scales = []
        for j in range(0, 8, 2):
            d, low, e = S[j][j], S[j + 1][j], S[j + 1][j + 1]
            det = d * e - low * low
            r = lax.rsqrt(d)
            rd = lax.rsqrt(det)
            q = rd * r
            r1 = q * d
            for i in range(j + 2, 8):
                S[i][j + 1] = (S[i][j + 1] * d - low * S[i][j]) * q
                S[i][j] = S[i][j] * r
            S[j + 1][j] = low * r
            for i in range(j + 2, 8):
                for c in range(j + 2, i + 1):
                    S[i][c] = (S[i][c] - S[i][j] * S[c][j]) - S[i][j + 1] * S[c][j + 1]
            scales += [r, r1]
            rows[j] = rows[j] * r
            rows[j + 1] = (rows[j + 1] - S[j + 1][j] * rows[j]) * r1
            for i in range(j + 2, 8):
                rows[i] = (rows[i] - S[i][j] * rows[j]) - S[i][j + 1] * rows[j + 1]
        return scales
    def pivot_of(s):
        return (lane8 >= s * G) & (lane8 < s * G + G)

    def eliminate(s, R, groups):
        for g in groups:
            index = sub8 + 8 * g
            acc = jnp.where(pivot_of(s), 0.0, d_ref[8 * g:8 * g + 8, :])
            for j in range(G):
                acc = acc - gather(R[j], index) * R[j]
            d_ref[8 * g:8 * g + 8, :] = acc

    def gather(x, index):
        return jnp.take_along_axis(x, index, axis=1, mode="promise_in_bounds")
    def begin(par, p0, p1, base):
        for c in range(8): v_ref[par, 0, c] = spread(p0, base + c)
        for c in range(16): v_ref[par, 3 + c // 8, c % 8] = spread(p1, base + c)
    def chain(s):
        base = s * G; par = s % 2; nxt = 1 - par; pivot = pivot_of(s)
        S = [[row(v_ref.at[par, 0, c], i) for c in range(i + 1)] for i in range(8)]
        V = [v_ref[par, 3 + c // 8, c % 8] for c in range(16)]
        x0 = jnp.where(pivot, (lane8 == base + sub8).astype(f32), d_ref[base:base + 8, :])
        x1 = jnp.where(pivot, (lane8 == base + 8 + sub8).astype(f32), d_ref[base + 8:base + 16, :])
        x_ref[par, 0] = x0
        R = [row(x_ref.at[par, 0], i) for i in range(8)]
        scales = chol8(S, R)
        for j in range(8):
            V[j] = V[j] * scales[j]
            for c in range(j + 1, 8): V[c] = V[c] - V[j] * S[c][j]
            v_ref[par, 1, j] = V[j]
            x1 = x1 - V[j] * R[j]
            for c in range(8): V[8 + c] = V[8 + c] - V[j] * row(v_ref.at[par, 1, j], c)
        for c in range(8): v_ref[par, 2, c] = V[8 + c]
        x_ref[par, 1] = x1
        S1 = [[row(v_ref.at[par, 2, c], i) for c in range(i + 1)] for i in range(8)]
        R1 = [row(x_ref.at[par, 1], i) for i in range(8)]
        more = s + 1 < steps
        if more:
            nb = base + G
            i0, i1 = sub8 + nb, sub8 + nb + 8
            q0 = jnp.where(pivot, 0.0, d_ref[nb:nb + 8, :]); q1 = jnp.where(pivot, 0.0, d_ref[nb + 8:nb + 16, :])
            for j in range(8):
                q0 = q0 - gather(R[j], i0) * R[j]
                q1 = q1 - gather(R[j], i1) * R[j]
            N0 = [spread(q0, nb + c) for c in range(8)]
            N1 = [spread(q1, nb + c) for c in range(16)]
        chol8(S1, R1)
        for i in range(8):
            w_ref[base + i:base + i + 1, :] = R[i][0:1, :]
            w_ref[base + 8 + i:base + 9 + i, :] = R1[i][0:1, :]
        if more:
            for j in range(8):
                m0, m1 = gather(R1[j], i0), gather(R1[j], i1)
                q0 = q0 - m0 * R1[j]
                q1 = q1 - m1 * R1[j]
                n_ref[j, 0] = m0
                n_ref[j, 1] = m1
                for c in range(8):
                    e0, e1 = row(n_ref.at[j, 0], c), row(n_ref.at[j, 1], c)
                    N0[c] = N0[c] - m0 * e0
                    N1[c] = N1[c] - m1 * e0
                    N1[8 + c] = N1[8 + c] - m1 * e1
            d_ref[nb:nb + 8, :] = q0
            d_ref[nb + 8:nb + 16, :] = q1
            for c in range(8): v_ref[nxt, 0, c] = N0[c]
            for c in range(16): v_ref[nxt, 3 + c // 8, c % 8] = N1[c]
    def near2(s):
        R = [row(w_ref, s * G + i) for i in range(G)]
        eliminate(s, R, (2 * s + 4, 2 * s + 5))
    def distant(s):
        lo = (s + 3) * G
        if lo >= B: return
        parts = thirds(w_ref[s * G:s * G + G, :])
        left = jnp.concatenate([parts[i] for i in (0, 0, 1, 1, 0, 2)], axis=0)
        right = jnp.concatenate([parts[i] for i in (0, 1, 0, 1, 2, 0)], axis=0)
        upd = lax.dot_general(left, right, (((0,), (0,)), ((), ())), preferred_element_type=f32)
        keep = (lane8[:1] < s * G) | (lane8[:1] >= s * G + G)
        d_ref[lo:, :] = jnp.where(keep, d_ref[lo:, :], 0.0) - upd[lo:]
    left_order = (0, 0, 1, 1, 0, 2)
    right_order = (0, 1, 0, 1, 2, 0)

    def left_of(parts):
        return jnp.concatenate([parts[i] for i in left_order], axis=1)

    def right_of(parts):
        return jnp.concatenate([parts[i] for i in right_order], axis=0)

    def panel(t, lo, hi):
        left = left_of([w3_ref[i] for i in range(3)])
        right = right_of(thirds(a_ref[t * B:(t + 1) * B, lo * B:hi * B]))
        p = jnp.dot(left, right, preferred_element_type=f32)
        if hi == nblk + 1:
            z_ref[t * B:(t + 1) * B, :] = p[:, -B:]
        if t + 1 == nblk:
            return
        for i, part in enumerate(thirds(p)):
            p3_ref[i, :, lo * B:hi * B] = part
        for c in range(lo, min(hi, nblk)):
            for i, part in enumerate(thirds(p[:, (c - lo) * B:(c - lo + 1) * B].T)):
                pt_ref[i, c * B:(c + 1) * B, :] = part

    def trailing(j, lo, hi):
        left = left_of([pt_ref[i, j * B:(j + 1) * B, :] for i in range(3)])
        right = right_of([p3_ref[i, :, lo * B:hi * B] for i in range(3)])
        return jnp.dot(left, right, preferred_element_type=f32)

    def update(j, lo, hi):
        a_ref[j * B:(j + 1) * B, lo * B:hi * B] = a_ref[j * B:(j + 1) * B, lo * B:hi * B] - trailing(j, lo, hi)

    build(0, (0,))
    d_ref[...] = a_ref[:B, :B]
    always = chol_id >= 0
    for k in range(nblk):
        for s in range(steps):
            @pl.when(always)
            def _(k=k, s=s):
                if s == 0:
                    begin(0, d_ref[0:8, :], d_ref[8:16, :], 0)
                if s and s + 1 < steps:
                    near2(s - 1)
                if s:
                    distant(s - 1)
                if k == 0:
                    if s < nblk:
                        build(s, range(max(s, 1), nblk))
                elif s == 0:
                    panel(k - 1, k + 1, nblk + 1)
                elif k + s - 1 < nblk:
                    j = k + s - 1
                    update(j, max(j, k + 1), nblk + 1)
                chain(s)
        for i, part in enumerate(thirds(jnp.where(lane <= sub, w_ref[...], 0.0))):
            w3_ref[i] = part
        if k == nc:
            m_ref[...] = -a_ref[cond:, total:]
        panel(k, k + 1, k + 2)
        if k + 1 < nblk:
            d_ref[...] = a_ref[(k + 1) * B:(k + 2) * B, (k + 1) * B:(k + 2) * B] - trailing(k + 1, k + 1, k + 2)

    out = mean_ref.shape[1]
    start = pl.multiple_of(chol_id * out, 8)
    pad = jnp.zeros((B - out, B), f32)
    mt = jnp.concatenate([m_ref[pl.ds(start, out), :], pad], axis=0).T
    zt = jnp.concatenate([z_ref[pl.ds(cond + start, out), :], pad], axis=0).T
    mean_ref[...] = mt[cols:2 * cols, :out]
    white_ref[...] = zt[:cols, :out]


def on_device(leaves, chols, coords, observed, cond_index):
    own = coords.shape[1]
    cond = cond_index.shape[1]
    cols = observed.shape[0]
    packed = jnp.concatenate([coords, observed], axis=0)
    out = own // chols
    total = own + cond
    bits = leaves.bit_length() - 1
    masks = tuple((1 << t) ^ (1 << (t - 1) if t > 1 else 0) for t in range(bits))
    grouped = 2 * cond // leaves % B == 0
    labels = [0]
    if grouped:
        pieces = [packed]
        def swap(even, odd):
            return [(j * chols + c, (j ^ (odd if c % 2 else even)) * chols + c)
                    for j in range(leaves) for c in range(chols) if (odd if c % 2 else even)]
        plan = [(m + (m >> 1 & 1), m + 1 - (m >> 1 & 1)) for m in range(0, leaves, 2)]
        got = [lax.ppermute(packed, ("leaf", "chol"), swap(*p)) for p in plan]
        cross = [(j, j ^ 1) for j in range(chols)]
        pieces += got + [lax.ppermute(g, "chol", cross) for g in got]
        labels = [0] + [p[0] + 256 * p[1] for p in plan] + [p[1] + 256 * p[0] for p in plan]
        rows = -(-packed.shape[0] // 8) * 8
    else:
        every = packed
        for mask in masks:
            swap = [(j, j ^ mask) for j in range(leaves)]
            every = jnp.concatenate([every, lax.ppermute(every, "leaf", swap)], axis=1)
        far = cond_index[0] // own ^ lax.axis_index("leaf")
        place = jnp.zeros_like(far)
        for bit in range(bits - 1, -1, -1):
            has = (far >> bit) & 1
            place = place + (has << bit)
            far = far ^ (has * masks[bit])
        pieces = [packed, jnp.take(every, place * own + cond_index[0] % own, axis=1)]
        rows = 8
    return pl.pallas_call(
        functools.partial(kernel, "leaf", "chol", tuple(labels) if grouped else ()),
        out_shape=(jax.ShapeDtypeStruct((cols, out), f32),) * 2,
        in_specs=[pl.BlockSpec(memory_space=pltpu.SMEM)]
        + [pl.BlockSpec(memory_space=pltpu.VMEM)] * (1 + len(pieces)),
        out_specs=(pl.BlockSpec(memory_space=pltpu.VMEM),) * 2,
        scratch_shapes=[
            pltpu.VMEM((total, total + B), f32),
            pltpu.VMEM((B, B), f32),
            pltpu.VMEM((2, 5, 8, 8, B), f32),
            pltpu.VMEM((2, 2, 8, B), f32),
            pltpu.VMEM((B, B), f32),
            pltpu.VMEM((total, B), f32),
            pltpu.VMEM((own, B), f32),
            pltpu.VMEM((leaves + 1 if grouped else 1, rows, own), f32),
            pltpu.VMEM((8, total), f32),
            pltpu.VMEM((3, B, B), bf16),
            pltpu.VMEM((3, B, total + B), bf16),
            pltpu.VMEM((3, total, B), bf16),
            pltpu.VMEM((8, 2, 8, B), f32),
            pltpu.VMEM((total, B), f32),
        ],
        compiler_params=pltpu.CompilerParams(vmem_limit_bytes=48 << 20),
        name="vecchia",
    )(cond_index, cond_index, *pieces)


def solution(mesh):
    return jax.shard_map(
        functools.partial(on_device, mesh.shape["leaf"], mesh.shape["chol"]),
        mesh=mesh,
        in_specs=(P(None, "leaf"), P(None, "leaf"), P("leaf", None)),
        out_specs=(P(None, ("leaf", "chol")), P(None, ("leaf", "chol"))),
        check_vma=False,
    )
```

```python
import functools
import jax
import jax.numpy as jnp
from jax import lax
from jax.experimental import pallas as pl
from jax.experimental.pallas import tpu as pltpu
from jax.sharding import PartitionSpec as P

length_scale = 0.3
nugget = 0.2
B = 128
G = 16
LANES = 128
f32 = jnp.float32
bf16 = jnp.bfloat16


def thirds(x):
    high = x.astype(bf16)
    rest = x - high.astype(f32)
    mid = rest.astype(bf16)
    return high, mid, (rest - mid.astype(f32)).astype(bf16)


def kernel(leaf_axis, chol_axis, masks, pos_ref, idx_ref, *refs):
    npieces = len(refs) - 16
    piece_refs = refs[:npieces]
    (mean_ref, white_ref, a_ref, d_ref, v_ref, x_ref, w_ref, z_ref, m_ref,
     g_ref, f_ref, w3_ref, p3_ref, pt_ref, n_ref, q_ref) = refs[npieces:]
    own_ref = piece_refs[0]
    own = own_ref.shape[1]
    cond = idx_ref.shape[1]
    cols = own_ref.shape[0] - 3
    total = cond + own
    nblk = total // B
    nc = cond // B
    leaf_id = lax.axis_index(leaf_axis)
    chol_id = lax.axis_index(chol_axis)

    lane = lax.broadcasted_iota(jnp.int32, (B, B), 1)
    sub = lax.broadcasted_iota(jnp.int32, (B, B), 0)

    if masks:
        i = 0
        for piece in piece_refs:
            tail = g_ref.shape[1] - piece.shape[0]
            for lo in range(0, piece.shape[1], own):
                g_ref[i] = jnp.concatenate([piece[:, lo:lo + own], jnp.zeros((tail, own), f32)], axis=0)
                i += 1
    row_form = []
    c0 = 2 * cols
    for k in range(nblk):
        if k < nc:
            if masks:
                far = pos_ref[0, k * B] // own ^ leaf_id
                place = 0
                for i, mask in enumerate(masks):
                    if i:
                        here = jnp.where(chol_id % 2 == 0, mask % 256, mask // 256)
                        place = jnp.where((far == here) & (here > 0), i, place)
                site = idx_ref[:, k * B:(k + 1) * B] % own
                hot = (lax.broadcasted_iota(jnp.int32, (own, B), 0) == site).astype(f32).astype(bf16)
                parts = jnp.dot(jnp.concatenate(thirds(g_ref[place]), axis=0), hot, preferred_element_type=f32)
                third = parts.shape[0] // 3
                blk = parts[:third] + parts[third:2 * third] + parts[2 * third:]
                blk = blk[:cols + 3]
            else:
                blk = piece_refs[1][:, k * B:(k + 1) * B]
            alive = (idx_ref[:, k * B:(k + 1) * B] // own != leaf_id).astype(f32)
            vals = blk[3:] * alive
            vals2 = vals
            away = (lax.broadcasted_iota(jnp.int32, (1, B), 1) + (k * B + 2)).astype(f32) * 1e3
            pts = jnp.where(alive > 0.5, blk[:3], away)
        else:
            blk = own_ref[:, (k - nc) * B:(k - nc + 1) * B]
            alive = jnp.ones((1, B), f32)
            vals = blk[3:]
            vals2 = jnp.zeros_like(vals)
            pts = blk[:3]
        stack = jnp.concatenate(
            [vals, vals2, pts, jnp.zeros((B - c0 - 3, B), f32)], axis=0)
        t = stack.T
        f_ref[:, k * B:(k + 1) * B] = jnp.concatenate([pts, alive, jnp.zeros((4, B), f32)], axis=0)
        a_ref[k * B:(k + 1) * B, total:] = jnp.where(lane < c0, t, 0.0)
        q_ref[k * B:(k + 1) * B, :] = t

    def build(k, tiles):
        t = q_ref[k * B:(k + 1) * B, :]
        cx, cy, cz = (jnp.broadcast_to(t[:, c0 + i:c0 + i + 1], (B, B)) for i in range(3))
        for c in tiles:
            rx, ry, rz, ra = (f_ref[i:i + 1, c * B:(c + 1) * B] for i in range(4))
            dx, dy, dz = cx - rx, cy - ry, cz - rz
            sq = jnp.maximum(dx * dx + dy * dy + dz * dz, 1e-30)
            kern = jnp.exp2(sq * lax.rsqrt(sq) * (-1.4426950408889634 / length_scale))
            if c == k:
                kern = jnp.where(lane == sub, kern + nugget * ra, kern)
            a_ref[k * B:(k + 1) * B, c * B:(c + 1) * B] = kern

    lane8 = lax.broadcasted_iota(jnp.int32, (8, B), 1)
    sub8 = lax.broadcasted_iota(jnp.int32, (8, B), 0)
    steps = B // G

    def spread(x, i):
        return jnp.broadcast_to(x[:, i:i + 1], (8, B))

    def row(ref, i):
        return jnp.broadcast_to(ref[i:i + 1, :], (8, B))

    def chol8(S, rows):
        scales = []
        for j in range(0, 8, 2):
            d, low, e = S[j][j], S[j + 1][j], S[j + 1][j + 1]
            det = d * e - low * low
            r = lax.rsqrt(d)
            rd = lax.rsqrt(det)
            q = rd * r
            r1 = q * d
            for i in range(j + 2, 8):
                S[i][j + 1] = (S[i][j + 1] * d - low * S[i][j]) * q
                S[i][j] = S[i][j] * r
            S[j + 1][j] = low * r
            for i in range(j + 2, 8):
                for c in range(j + 2, i + 1):
                    S[i][c] = (S[i][c] - S[i][j] * S[c][j]) - S[i][j + 1] * S[c][j + 1]
            scales += [r, r1]
            rows[j] = rows[j] * r
            rows[j + 1] = (rows[j + 1] - S[j + 1][j] * rows[j]) * r1
            for i in range(j + 2, 8):
                rows[i] = (rows[i] - S[i][j] * rows[j]) - S[i][j + 1] * rows[j + 1]
        return scales
    def pivot_of(s):
        return (lane8 >= s * G) & (lane8 < s * G + G)

    def eliminate(s, R, groups):
        for g in groups:
            index = sub8 + 8 * g
            acc = jnp.where(pivot_of(s), 0.0, d_ref[8 * g:8 * g + 8, :])
            for j in range(G):
                acc = acc - gather(R[j], index) * R[j]
            d_ref[8 * g:8 * g + 8, :] = acc

    def gather(x, index):
        return jnp.take_along_axis(x, index, axis=1, mode="promise_in_bounds")
    def begin(par, p0, p1, base):
        for c in range(8): v_ref[par, 0, c] = spread(p0, base + c)
        for c in range(16): v_ref[par, 3 + c // 8, c % 8] = spread(p1, base + c)
    def chain(s):
        base = s * G; par = s % 2; nxt = 1 - par; pivot = pivot_of(s)
        S = [[row(v_ref.at[par, 0, c], i) for c in range(i + 1)] for i in range(8)]
        V = [v_ref[par, 3 + c // 8, c % 8] for c in range(16)]
        x0 = jnp.where(pivot, (lane8 == base + sub8).astype(f32), d_ref[base:base + 8, :])
        x1 = jnp.where(pivot, (lane8 == base + 8 + sub8).astype(f32), d_ref[base + 8:base + 16, :])
        x_ref[par, 0] = x0
        R = [row(x_ref.at[par, 0], i) for i in range(8)]
        scales = chol8(S, R)
        for j in range(8):
            V[j] = V[j] * scales[j]
            for c in range(j + 1, 8): V[c] = V[c] - V[j] * S[c][j]
            v_ref[par, 1, j] = V[j]
            x1 = x1 - V[j] * R[j]
            for c in range(8): V[8 + c] = V[8 + c] - V[j] * row(v_ref.at[par, 1, j], c)
        for c in range(8): v_ref[par, 2, c] = V[8 + c]
        x_ref[par, 1] = x1
        S1 = [[row(v_ref.at[par, 2, c], i) for c in range(i + 1)] for i in range(8)]
        R1 = [row(x_ref.at[par, 1], i) for i in range(8)]
        more = s + 1 < steps
        if more:
            nb = base + G
            i0, i1 = sub8 + nb, sub8 + nb + 8
            q0 = jnp.where(pivot, 0.0, d_ref[nb:nb + 8, :]); q1 = jnp.where(pivot, 0.0, d_ref[nb + 8:nb + 16, :])
            for j in range(8):
                q0 = q0 - gather(R[j], i0) * R[j]
                q1 = q1 - gather(R[j], i1) * R[j]
            N0 = [spread(q0, nb + c) for c in range(8)]
            N1 = [spread(q1, nb + c) for c in range(16)]
        chol8(S1, R1)
        for i in range(8):
            w_ref[base + i:base + i + 1, :] = R[i][0:1, :]
            w_ref[base + 8 + i:base + 9 + i, :] = R1[i][0:1, :]
        if more:
            for j in range(8):
                m0, m1 = gather(R1[j], i0), gather(R1[j], i1)
                q0 = q0 - m0 * R1[j]
                q1 = q1 - m1 * R1[j]
                n_ref[j, 0] = m0
                n_ref[j, 1] = m1
                for c in range(8):
                    e0, e1 = row(n_ref.at[j, 0], c), row(n_ref.at[j, 1], c)
                    N0[c] = N0[c] - m0 * e0
                    N1[c] = N1[c] - m1 * e0
                    N1[8 + c] = N1[8 + c] - m1 * e1
            d_ref[nb:nb + 8, :] = q0
            d_ref[nb + 8:nb + 16, :] = q1
            for c in range(8): v_ref[nxt, 0, c] = N0[c]
            for c in range(16): v_ref[nxt, 3 + c // 8, c % 8] = N1[c]
    def near2(s):
        R = [row(w_ref, s * G + i) for i in range(G)]
        eliminate(s, R, (2 * s + 4, 2 * s + 5))
    def distant(s):
        lo = (s + 3) * G
        if lo >= B: return
        parts = thirds(w_ref[s * G:s * G + G, :])
        left = jnp.concatenate([parts[i] for i in (0, 0, 1, 1, 0, 2)], axis=0)
        right = jnp.concatenate([parts[i] for i in (0, 1, 0, 1, 2, 0)], axis=0)
        upd = lax.dot_general(left, right, (((0,), (0,)), ((), ())), preferred_element_type=f32)
        keep = (lane8[:1] < s * G) | (lane8[:1] >= s * G + G)
        d_ref[lo:, :] = jnp.where(keep, d_ref[lo:, :], 0.0) - upd[lo:]
    left_order = (0, 0, 1, 1, 0, 2)
    right_order = (0, 1, 0, 1, 2, 0)

    def left_of(parts):
        return jnp.concatenate([parts[i] for i in left_order], axis=1)

    def right_of(parts):
        return jnp.concatenate([parts[i] for i in right_order], axis=0)

    def panel(t, lo, hi):
        left = left_of([w3_ref[i] for i in range(3)])
        right = right_of(thirds(a_ref[t * B:(t + 1) * B, lo * B:hi * B]))
        p = jnp.dot(left, right, preferred_element_type=f32)
        if hi == nblk + 1:
            z_ref[t * B:(t + 1) * B, :] = p[:, -B:]
        if t + 1 == nblk:
            return
        for i, part in enumerate(thirds(p)):
            p3_ref[i, :, lo * B:hi * B] = part
        for c in range(lo, min(hi, nblk)):
            for i, part in enumerate(thirds(p[:, (c - lo) * B:(c - lo + 1) * B].T)):
                pt_ref[i, c * B:(c + 1) * B, :] = part

    def trailing(j, lo, hi):
        left = left_of([pt_ref[i, j * B:(j + 1) * B, :] for i in range(3)])
        right = right_of([p3_ref[i, :, lo * B:hi * B] for i in range(3)])
        return jnp.dot(left, right, preferred_element_type=f32)

    def update(j, lo, hi):
        a_ref[j * B:(j + 1) * B, lo * B:hi * B] = a_ref[j * B:(j + 1) * B, lo * B:hi * B] - trailing(j, lo, hi)

    build(0, (0,))
    d_ref[...] = a_ref[:B, :B]
    for k in range(nblk):
        for s in range(steps):
            with jax.named_scope("step"):
                if s == 0:
                    begin(0, d_ref[0:8, :], d_ref[8:16, :], 0)
                if s and s + 1 < steps:
                    near2(s - 1)
                if s:
                    distant(s - 1)
                if k == 0:
                    if s < nblk:
                        build(s, range(max(s, 1), nblk))
                elif s == 0:
                    panel(k - 1, k + 1, nblk + 1)
                elif k + s - 1 < nblk:
                    j = k + s - 1
                    update(j, max(j, k + 1), nblk + 1)
                chain(s)
        for i, part in enumerate(thirds(jnp.where(lane <= sub, w_ref[...], 0.0))):
            w3_ref[i] = part
        if k == nc:
            m_ref[...] = -a_ref[cond:, total:]
        panel(k, k + 1, k + 2)
        if k + 1 < nblk:
            d_ref[...] = a_ref[(k + 1) * B:(k + 2) * B, (k + 1) * B:(k + 2) * B] - trailing(k + 1, k + 1, k + 2)

    out = mean_ref.shape[1]
    start = pl.multiple_of(chol_id * out, 8)
    pad = jnp.zeros((B - out, B), f32)
    mt = jnp.concatenate([m_ref[pl.ds(start, out), :], pad], axis=0).T
    zt = jnp.concatenate([z_ref[pl.ds(cond + start, out), :], pad], axis=0).T
    mean_ref[...] = mt[cols:2 * cols, :out]
    white_ref[...] = zt[:cols, :out]


def on_device(leaves, chols, coords, observed, cond_index):
    own = coords.shape[1]
    cond = cond_index.shape[1]
    cols = observed.shape[0]
    packed = jnp.concatenate([coords, observed], axis=0)
    out = own // chols
    total = own + cond
    bits = leaves.bit_length() - 1
    masks = tuple((1 << t) ^ (1 << (t - 1) if t > 1 else 0) for t in range(bits))
    grouped = 2 * cond // leaves % B == 0
    labels = [0]
    if grouped:
        pieces = [packed]
        def swap(even, odd):
            return [(j * chols + c, (j ^ (odd if c % 2 else even)) * chols + c)
                    for j in range(leaves) for c in range(chols) if (odd if c % 2 else even)]
        plan = [(m + (m >> 1 & 1), m + 1 - (m >> 1 & 1)) for m in range(0, leaves, 2)]
        got = [lax.ppermute(packed, ("leaf", "chol"), swap(*p)) for p in plan]
        cross = [(j, j ^ 1) for j in range(chols)]
        pieces += got + [lax.ppermute(g, "chol", cross) for g in got]
        labels = [0] + [p[0] + 256 * p[1] for p in plan] + [p[1] + 256 * p[0] for p in plan]
        rows = -(-packed.shape[0] // 8) * 8
    else:
        every = packed
        for mask in masks:
            swap = [(j, j ^ mask) for j in range(leaves)]
            every = jnp.concatenate([every, lax.ppermute(every, "leaf", swap)], axis=1)
        far = cond_index[0] // own ^ lax.axis_index("leaf")
        place = jnp.zeros_like(far)
        for bit in range(bits - 1, -1, -1):
            has = (far >> bit) & 1
            place = place + (has << bit)
            far = far ^ (has * masks[bit])
        pieces = [packed, jnp.take(every, place * own + cond_index[0] % own, axis=1)]
        rows = 8
    return pl.pallas_call(
        functools.partial(kernel, "leaf", "chol", tuple(labels) if grouped else ()),
        out_shape=(jax.ShapeDtypeStruct((cols, out), f32),) * 2,
        in_specs=[pl.BlockSpec(memory_space=pltpu.SMEM)]
        + [pl.BlockSpec(memory_space=pltpu.VMEM)] * (1 + len(pieces)),
        out_specs=(pl.BlockSpec(memory_space=pltpu.VMEM),) * 2,
        scratch_shapes=[
            pltpu.VMEM((total, total + B), f32),
            pltpu.VMEM((B, B), f32),
            pltpu.VMEM((2, 5, 8, 8, B), f32),
            pltpu.VMEM((2, 2, 8, B), f32),
            pltpu.VMEM((B, B), f32),
            pltpu.VMEM((total, B), f32),
            pltpu.VMEM((own, B), f32),
            pltpu.VMEM((leaves + 1 if grouped else 1, rows, own), f32),
            pltpu.VMEM((8, total), f32),
            pltpu.VMEM((3, B, B), bf16),
            pltpu.VMEM((3, B, total + B), bf16),
            pltpu.VMEM((3, total, B), bf16),
            pltpu.VMEM((8, 2, 8, B), f32),
            pltpu.VMEM((total, B), f32),
        ],
        compiler_params=pltpu.CompilerParams(vmem_limit_bytes=48 << 20),
        name="vecchia",
    )(cond_index, cond_index, *pieces)


def solution(mesh):
    return jax.shard_map(
        functools.partial(on_device, mesh.shape["leaf"], mesh.shape["chol"]),
        mesh=mesh,
        in_specs=(P(None, "leaf"), P(None, "leaf"), P("leaf", None)),
        out_specs=(P(None, ("leaf", "chol")), P(None, ("leaf", "chol"))),
        check_vma=False,
    )
```
